32 devices in a mesh: dp: 4 (over y, x), expert: 8 (over z, core).
Axes of the slice: x: 2, y: 2, z: 4, core: 2. Of those that a mesh axis runs over, the one named last changes fastest.
Arguments:
- features: float32 [32768, 256], P(('dp', 'expert')), may hold values from -6 to 6
- cotangent: float32 [32768, 512], P(('dp', 'expert')), may hold values from -6 to 6
- routes: int32 [32768, 8], P(('dp', 'expert')), may hold values from 0 to 15, all different within a row; in each aligned block of 256 rows (0 to 255, 256 to 511, ...) at most 192 rows name the same one
- lengths: int32 [32, 16], P(('dp', 'expert')), may hold values from 1 to 200, 1024 in all within a row
- gate_weight: float32 [256, 40], replicated, may hold values from -0.1875 to 0.1875
- first_weight: float32 [16, 256, 256], P('expert', 'dp'), may hold values from -0.375 to 0.375
- second_weight: float32 [16, 256, 256], P('expert', 'dp'), may hold values from -0.75 to 0.75
- expert_bias: float32 [16, 512], P('expert', 'dp'), may hold values from -0.625 to 0.625
- gate_momentum: float32 [256, 40], replicated, may hold values from -12 to 12
- gate_average: float32 [256, 40], replicated, may hold values from -0.1875 to 0.1875
- first_momentum: float32 [16, 256, 256], P('expert', 'dp'), may hold values from -1.25 to 1.25
- first_average: float32 [16, 256, 256], P('expert', 'dp'), may hold values from -0.375 to 0.375
- second_momentum: float32 [16, 256, 256], P('expert', 'dp'), may hold values from -0.625 to 0.625
- second_average: float32 [16, 256, 256], P('expert', 'dp'), may hold values from -0.75 to 0.75
- bias_momentum: float32 [16, 512], P('expert', 'dp'), may hold values from -1.25 to 1.25
- bias_average: float32 [16, 512], P('expert', 'dp'), may hold values from -0.625 to 0.625
Outputs:
- task_outputs: float32 [32768, 512], P(('dp', 'expert'))
- input_grad: float32 [32768, 256], P(('dp', 'expert'))
- gate_momentum_new: float32 [256, 40], replicated
- gate_weight_new: float32 [256, 40], replicated
- gate_average_new: float32 [256, 40], replicated
- first_momentum_new: float32 [16, 256, 256], P('expert', 'dp')
- first_weight_new: float32 [16, 256, 256], P('expert', 'dp')
- first_average_new: float32 [16, 256, 256], P('expert', 'dp')
- second_momentum_new: float32 [16, 256, 256], P('expert', 'dp')
- second_weight_new: float32 [16, 256, 256], P('expert', 'dp')
- second_average_new: float32 [16, 256, 256], P('expert', 'dp')
- bias_momentum_new: float32 [16, 512], P('expert', 'dp')
- bias_new: float32 [16, 512], P('expert', 'dp')
- bias_average_new: float32 [16, 512], P('expert', 'dp')
The draws below stay inside these ranges and needn't reach their ends.
Inputs may be any that keep to these rules, and one draw needn't show every extreme that they name: `routes`: each row names 8 different experts: the first 4 are task 0's selectors, the next 4 task 1's. In each aligned block of 256 rows (one micro-batch of one device) no expert is named by more than 192 rows, and in some block one expert is named by exactly 192 rows. `lengths`: the sessions of one device cover its 1024 rows in order and never cross devices; the longest has the maximum length.
All inputs are finite; a program needn't handle non-finite values.
Results may differ from the reference program's by a relative error of at most 0.002.
Values sent between devices are 32-bit elements; how exact they have to be, the bound alone decides.
A program may use at most 192 MiB of HBM per device.

```python
import math
import jax
import jax.numpy as jnp
import numpy as np
from jax import lax

D = 256
HID = 256
DOUT = 256
EXPERTS = 16
BITS = 4
TASKS = 2
SELECT = 4
SESS_MAX = 200
MICRO = 4
ROWS_DEV = 1024
MB = 256
CAP = 192
SESS_DEV = 16
ROWS = 32768
N_DP = 4
N_EXPERT = 8


def block_scale(rng, extent, cuts, low, largest):
    gain, own = 1.0, jax.random.fold_in(rng, 6)
    for axis_at, shards_of in cuts:
        steps = jnp.exp(jax.random.uniform(jax.random.fold_in(own, axis_at), (shards_of,), jnp.float32, low / len(cuts), largest / len(cuts)))
        gain = gain * jnp.repeat(steps, extent[axis_at] // shards_of).reshape([-1 if axis == axis_at else 1 for axis in range(len(extent))])
    return gain


def profile(count, total, reach, slope):
    portions = [(1 << 20) // math.isqrt(grade ** slope) + 1 for grade in range(2, count + 1)]
    surplus, given = total - reach - (count - 1), [1] * (count - 1)
    while surplus > 0:
        movable = [i for i in range(count - 1) if given[i] < reach]
        pool, remaining = sum([portions[i] for i in movable]), surplus
        for i in movable:
            extra = min(reach - given[i], max(1, remaining * portions[i] // pool), surplus)
            given[i] = given[i] + extra
            surplus = surplus - extra
    return np.array([reach] + given)


def uneven_parts(stream_key, count, total, most, skew):
    if count == 2:
        one = jax.random.randint(stream_key, (), max(1, total - most), min(most, total - 1) + 1)
        return jnp.stack([one, total - one])
    sizes = jnp.asarray(profile(count, total, most, skew), jnp.int32)
    pairs = (count - 1) // 2
    giver, receiver = sizes[1:1 + 2 * pairs:2], sizes[2:2 + 2 * pairs:2]
    slack = jnp.minimum(giver - 1, most - receiver)
    passed = jax.random.randint(jax.random.fold_in(stream_key, 1), (pairs,), 0, 1 << 20) % (slack + 1)
    sizes = sizes.at[1:1 + 2 * pairs:2].set(giver - passed).at[2:2 + 2 * pairs:2].set(receiver + passed)
    return sizes[jax.random.permutation(jax.random.fold_in(stream_key, 2), count)]


def deal_out(key, own, number, rows, number_of, top, most, slope):
    sequence = jax.random.permutation(key, number_of)
    crowded, ordinary = portions_of(number_of, rows * top, most, slope, True), portions_of(number_of, rows * top, most, slope, False)
    places = jnp.arange(number_of)

    def named(sizes, offset_by):
        used = int((sizes > 0).sum())
        fixed = max(1, used // 4)
        moved = fixed + (places - fixed + offset_by * (used - fixed)) % max(1, number_of - fixed)
        return jnp.zeros((number_of,), jnp.int32).at[sequence[jnp.where(places < fixed, places, moved)]].set(jnp.asarray(sizes, jnp.int32))

    sizes = jnp.where(number % 4 == 0, named(crowded, number // 4), named(ordinary, number - number // 4 - 1))
    mixed = jax.random.permutation(jax.random.fold_in(own, 3), number_of)
    giver, taker = mixed[0:number_of // 2 * 2:2], mixed[1:number_of // 2 * 2:2]
    slack = jnp.minimum(sizes[giver] - 1, most - sizes[taker]) // 2
    slack = jnp.where((giver == sequence[0]) | (taker == sequence[0]) | (sizes[taker] == 0), 0, jnp.maximum(slack, 0))
    moved = jax.random.randint(jax.random.fold_in(own, 4), (number_of // 2,), 0, 1 << 20) % (slack + 1)
    sizes = sizes.at[giver].add(-moved).at[taker].add(moved)
    labels = jnp.searchsorted(jnp.cumsum(sizes), jnp.arange(rows * top), side="right").astype(jnp.int32)
    table = labels.reshape(top, rows).T
    table = table[jax.random.permutation(jax.random.fold_in(own, 1), rows)]
    offset_by = jax.random.randint(jax.random.fold_in(own, 2), (rows, 1), 0, top)
    return jnp.take_along_axis(table, (jnp.arange(top)[None, :] + offset_by) % top, axis=1)


def portions_of(amount, total, most, slope, full):
    weights = [(1 << 20) // math.isqrt(standing ** slope) + 1 for standing in range(1, amount + 1)]
    largest = most if full else min(most, max(-(-total // amount), total * weights[0] // sum(weights)))
    least = 1 if total - largest >= amount - 1 else 0
    given, spare = [largest] + [least] * (amount - 1), total - largest - least * (amount - 1)
    while spare > 0:
        movable = [i for i in range(1, amount) if given[i] < largest] or [i for i in range(1, amount) if given[i] < most]
        whole, left = sum([weights[i] for i in movable]), spare
        for i in movable:
            extra = min(most - given[i], max(1, left * weights[i] // whole), spare)
            given[i] = given[i] + extra
            spare = spare - extra
    return np.array(given)


def normal_values(own_key, dims, scale, most, shards=(), kind=jnp.bfloat16):
    level = block_scale(own_key, dims, shards, -0.22, 0.18) if shards else 1.0
    values = jax.random.normal(own_key, dims, jnp.float32) * scale * level
    return jnp.minimum(jnp.maximum(values, -most), most).astype(kind)


def setup_inputs(seed: int = 0) -> dict:
    key_list = jax.random.split(jax.random.key(seed), 17)
    features = normal_values(key_list[0], (ROWS, D), 1.0, 6.0, ((0, 32),), jnp.float32)
    cotangent = normal_values(key_list[1], (ROWS, TASKS * DOUT), 1.0, 6.0, ((0, 32),), jnp.float32)
    routes_keys = jax.random.split(jax.random.fold_in(key_list[2], 1), ROWS // MB)
    routes_turns = jax.random.permutation(jax.random.fold_in(key_list[2], 3), ROWS // MB)
    routes = jax.vmap(lambda own, number: deal_out(jax.random.fold_in(key_list[2], 2), own, number, MB, EXPERTS, TASKS * SELECT, CAP, 2))(routes_keys, routes_turns).reshape((ROWS, TASKS * SELECT))
    lengths = jax.vmap(lambda own: uneven_parts(own, SESS_DEV, ROWS_DEV, min(SESS_MAX, ROWS_DEV // 2), 2))(jax.random.split(key_list[3], (N_DP * N_EXPERT))).reshape((N_DP * N_EXPERT, SESS_DEV)).astype(jnp.int32)
    gate_weight = normal_values(key_list[4], (D, TASKS * SELECT * (BITS + 1)), (4 * D) ** -0.5, 0.1875, (), jnp.float32)
    first_weight = normal_values(key_list[5], (EXPERTS, D, HID), D ** -0.5, 0.375, ((0, 8), (1, 4)), jnp.float32)
    second_weight = normal_values(key_list[6], (EXPERTS, HID, DOUT), (HID // 4) ** -0.5, 0.75, ((0, 8), (1, 4)), jnp.float32)
    expert_bias = normal_values(key_list[7], (EXPERTS, HID + DOUT), 0.1, 0.625, ((0, 8), (1, 4)), jnp.float32)
    gate_momentum = normal_values(key_list[8], (D, TASKS * SELECT * (BITS + 1)), 2.0, 12.0, (), jnp.float32)
    gate_average = normal_values(key_list[9], (D, TASKS * SELECT * (BITS + 1)), (4 * D) ** -0.5, 0.1875, (), jnp.float32)
    first_momentum = normal_values(key_list[10], (EXPERTS, D, HID), 0.2, 1.25, ((0, 8), (1, 4)), jnp.float32)
    first_average = normal_values(key_list[11], (EXPERTS, D, HID), D ** -0.5, 0.375, ((0, 8), (1, 4)), jnp.float32)
    second_momentum = normal_values(key_list[12], (EXPERTS, HID, DOUT), 0.1, 0.625, ((0, 8), (1, 4)), jnp.float32)
    second_average = normal_values(key_list[13], (EXPERTS, HID, DOUT), (HID // 4) ** -0.5, 0.75, ((0, 8), (1, 4)), jnp.float32)
    bias_momentum = normal_values(key_list[14], (EXPERTS, HID + DOUT), 0.2, 1.25, ((0, 8), (1, 4)), jnp.float32)
    bias_average = normal_values(key_list[15], (EXPERTS, HID + DOUT), 0.1, 0.625, ((0, 8), (1, 4)), jnp.float32)
    return {"features": features, "cotangent": cotangent, "routes": routes, "lengths": lengths, "gate_weight": gate_weight, "first_weight": first_weight, "second_weight": second_weight, "expert_bias": expert_bias, "gate_momentum": gate_momentum, "gate_average": gate_average, "first_momentum": first_momentum, "first_average": first_average, "second_momentum": second_momentum, "second_average": second_average, "bias_momentum": bias_momentum, "bias_average": bias_average}


HIGHEST = lax.Precision.HIGHEST
OFFSET = 3.5
SHARPNESS = 10.0
MOMENTUM = 0.5
AVERAGE_DECAY = 0.5
EXPERT_RATE = 0.4
GATE_RATE = 0.01

def smooth_step(argument):
    clipped = jnp.clip(argument, -0.5 * SHARPNESS, 0.5 * SHARPNESS)
    return -2.0 / SHARPNESS ** 3 * clipped ** 3 + 1.5 / SHARPNESS * clipped + 0.5

def gate_strengths(features, gate_weight, lengths_row, chosen):
    row_count = features.shape[0]
    session_ends = jnp.cumsum(lengths_row, dtype=jnp.int32)
    starts = session_ends - lengths_row
    places = jnp.arange(row_count, dtype=jnp.int32)[:, None]
    member = ((places >= starts[None, :]) & (places < session_ends[None, :])).astype(jnp.float32)
    session_sums = jnp.dot(member.T, features, precision=HIGHEST)
    session_means = session_sums / lengths_row.astype(jnp.float32)[:, None]
    context = features + jnp.dot(member, session_means, precision=HIGHEST)
    logits = jnp.dot(context, gate_weight, precision=HIGHEST).reshape(row_count, TASKS, SELECT, BITS + 1)
    weights = jax.nn.softmax(logits[..., 0], axis=-1)
    powers = 2 ** jnp.arange(BITS, dtype=jnp.int32)
    code_bits = chosen.reshape(row_count, TASKS, SELECT)[..., None] // powers % 2
    code_signs = 2.0 * code_bits.astype(jnp.float32) - 1.0
    strength = jnp.prod(smooth_step(code_signs * logits[..., 1:] + OFFSET), axis=-1)
    return (weights * strength).reshape(row_count, TASKS * SELECT)

def slot_index(chosen):
    destination = chosen.reshape(-1)
    matches = (destination[:, None] == jnp.arange(EXPERTS, dtype=jnp.int32)[None, :]).astype(jnp.int32)
    before = jnp.cumsum(matches, axis=0, dtype=jnp.int32) - matches
    position = lax.optimization_barrier(jnp.sum(before * matches, axis=1, dtype=jnp.int32))
    return destination * CAP + position

def expert_forward(slot_rows, first_full, second_full, bias_full):
    pre_act = jnp.einsum('sjcd,jdh->sjch', slot_rows, first_full, precision=HIGHEST) + bias_full[None, :, None, :HID]
    hidden = jax.nn.relu(pre_act)
    return jnp.einsum('sjch,jho->sjco', hidden, second_full, precision=HIGHEST) + bias_full[None, :, None, HID:]

def device_forward(features, lengths_row, chosen, gate_weight, first_full, second_full, bias_full):
    pair_count = TASKS * SELECT
    gate_terms = gate_strengths(features, gate_weight, lengths_row, chosen)
    slot_place = jax.vmap(slot_index)(chosen.reshape(MICRO, MB, pair_count))
    targets = slot_place // CAP
    position = slot_place % CAP
    micro_ids = jnp.arange(MICRO, dtype=jnp.int32)[:, None]
    destination = ((targets * MICRO + micro_ids) * CAP + position).reshape(-1)
    source = jnp.repeat(features, pair_count, axis=0)
    buffer = jnp.zeros((EXPERTS * MICRO * CAP, D), jnp.float32).at[destination].set(source)
    result = expert_forward(buffer.reshape(1, EXPERTS, MICRO * CAP, D), first_full, second_full, bias_full)
    picked = result.reshape(EXPERTS * MICRO * CAP, DOUT)[destination].reshape(ROWS_DEV, TASKS, SELECT, DOUT)
    combined = lax.optimization_barrier(jnp.sum(gate_terms.reshape(ROWS_DEV, TASKS, SELECT, 1) * picked, axis=2))
    return combined.reshape(ROWS_DEV, TASKS * DOUT)

def apply_update(weight, gradient, momentum, average, step_rate):
    momentum_new = MOMENTUM * momentum + gradient
    weight_new = weight - step_rate * (gradient + MOMENTUM * momentum_new)
    average_new = AVERAGE_DECAY * average + (1.0 - AVERAGE_DECAY) * weight_new
    return (momentum_new, weight_new, average_new)

def reference(features, cotangent, routes, lengths, gate_weight, first_weight, second_weight, expert_bias, gate_momentum, gate_average, first_momentum, first_average, second_momentum, second_average, bias_momentum, bias_average):
    devices = N_DP * N_EXPERT

    def forward(rows_all, gate_in, first_in, second_in, bias_in):

        def per_device(packed):
            shard_rows, lengths_row, chosen = packed
            return device_forward(shard_rows, lengths_row, chosen, gate_in, first_in, second_in, bias_in)
        combined = lax.map(jax.checkpoint(per_device), (rows_all.reshape(devices, ROWS_DEV, D), lengths, routes.reshape(devices, ROWS_DEV, TASKS * SELECT)))
        return combined.reshape(ROWS, TASKS * DOUT)
    task_outputs, pullback = jax.vjp(forward, features, gate_weight, first_weight, second_weight, expert_bias)
    input_grad, gate_grad, first_grad, second_grad, bias_grad = pullback(cotangent)
    grad_scale = 1.0 / math.sqrt(ROWS)
    gate_new = apply_update(gate_weight, gate_grad * grad_scale, gate_momentum, gate_average, GATE_RATE)
    first_new = apply_update(first_weight, first_grad * grad_scale, first_momentum, first_average, EXPERT_RATE)
    second_new = apply_update(second_weight, second_grad * grad_scale, second_momentum, second_average, EXPERT_RATE)
    bias_new = apply_update(expert_bias, bias_grad * grad_scale, bias_momentum, bias_average, EXPERT_RATE)
    return (task_outputs, input_grad, gate_new[0], gate_new[1], gate_new[2], first_new[0], first_new[1], first_new[2], second_new[0], second_new[1], second_new[2], bias_new[0], bias_new[1], bias_new[2])
```

```python
import functools
import math

import jax
import jax.numpy as jnp
from jax import lax
from jax.experimental import pallas as pl
from jax.experimental.pallas import tpu as pltpu
from jax.sharding import PartitionSpec as P

D = 256
HID = 256
DOUT = 256
EXPERTS = 16
BITS = 4
TASKS = 2
SELECT = 4
PAIRS = TASKS * SELECT
CORES = 2
TILE = 512
PIECES = 4

OFFSET = 3.5
SHARPNESS = 10.0
MOMENTUM = 0.5
AVERAGE_DECAY = 0.5
EXPERT_RATE = 0.4
GATE_RATE = 0.01
F32 = jnp.float32
BF16 = jnp.bfloat16
MESH = pl.DeviceIdType.MESH


def update(weight, gradient, momentum, average, step_rate):
    momentum_new = MOMENTUM * momentum + gradient
    weight_new = weight - step_rate * (gradient + MOMENTUM * momentum_new)
    average_new = AVERAGE_DECAY * average + (1.0 - AVERAGE_DECAY) * weight_new
    return (momentum_new, weight_new, average_new)


def mm(left, right):
    return jnp.dot(left, right, preferred_element_type=F32)


def split2(value):
    high = value.astype(BF16)
    return high, (value - high.astype(F32)).astype(BF16)


def split3(value):
    high = value.astype(BF16)
    rest = value - high.astype(F32)
    middle = rest.astype(BF16)
    return high, middle, (rest - middle.astype(F32)).astype(BF16)


def expert_kernel(
    dims,
    x_hbm,
    cot_hbm,
    routes_ref,
    lengths_ref,
    gw_ref,
    first_hbm,
    second_hbm,
    bias_ref,
    out_hbm,
    ig_hbm,
    gsum_ref,
    gg_ref,
    pack_ref,
    xin,
    cin,
    grb,
    xcat,
    xt,
    ccat,
    ct,
    gm,
    st,
    mt,
    acc,
    iga,
    s_gh,
    s_hc,
    s_w1,
    s_w1t,
    s_w2,
    s_w2t,
    bias,
    b1acc,
    b2grad,
    wbuf,
    gbuf,
    rbuf,
    psum,
    fbuf,
    ret_out,
    ret_ig,
    ret_gc,
    gcp,
    saved,
    ar_own,
    ar_sib,
    ar_dp,
    ar_z,
    local_sem,
    sib_send,
    sib_recv,
    z_send,
    z_recv,
    p_send,
    p_recv,
    a_send,
    a_recv,
    f_send,
    f_recv,
    r_send,
    r_recv,
):
    rows, n_dp, nz, per_device = dims
    count = nz * per_device
    part = D // n_dp
    lanes = 128
    kinds = BITS + 1
    both = CORES * rows
    relay = n_dp == 4
    width = 2 * HID // n_dp
    upper, lower = slice(0, part), slice(part, 2 * part + 8)
    dp = lax.axis_index("dp")
    place = lax.axis_index("expert")
    z = place // CORES
    core = place % CORES
    sibling = (dp, z * CORES + (1 - core))

    def peer(m):
        return ((dp + m) % n_dp, place)

    def plane(dz):
        return (dp, ((z + dz) % nz) * CORES + core)

    flip = (dp // 2) * 2 + (1 - dp % 2)
    turn = (1 - dp // 2) * 2 + dp % 2
    across = (n_dp - 1) - dp

    def slot(k):
        step = k + (per_device - 1)
        return (step // per_device) % nz, step % per_device

    def expert_of(k):
        dz, l = slot(k)
        return (((z + dz) % nz) * CORES + core) * per_device + l

    barrier = pltpu.get_barrier_semaphore()
    greet = [sibling] + [peer(m) for m in range(1, n_dp)] + [plane(dz) for dz in range(1, nz)]
    for other in greet:
        pl.semaphore_signal(barrier, inc=1, device_id=other, device_id_type=MESH)
    copies = [
        pltpu.make_async_copy(x_hbm, xin.at[0], local_sem.at[0]),
        pltpu.make_async_copy(cot_hbm, cin.at[0], local_sem.at[1]),
    ]
    loads = []
    for l in range(per_device):
        loads += [
            pltpu.make_async_copy(first_hbm.at[l], pack_ref.at[l, upper], local_sem.at[2 + 3 * l]),
            pltpu.make_async_copy(
                second_hbm.at[l], pack_ref.at[l, slice(part, 2 * part)], local_sem.at[3 + 3 * l]
            ),
        ]
    for copy in loads + copies:
        copy.start()
    spread_lane = lax.broadcasted_iota(jnp.int32, (1, HID), 1)
    bias_row, bias_lane = dp * width // HID, dp * width % HID
    for l in range(per_device):
        wide = jnp.concatenate([bias_ref[l : l + 1, :]] * (HID // width), axis=1)
        wide = jnp.where((spread_lane >= bias_lane) & (spread_lane < bias_lane + width), wide, 0.0)
        rows_of = lax.broadcasted_iota(jnp.int32, (8, HID), 0)
        pack_ref[l, 2 * part : 2 * part + 8, :] = jnp.where(rows_of == bias_row, wide, 0.0)
    for copy in loads:
        copy.wait()
    pl.semaphore_wait(barrier, len(greet))

    def remote(src, dst, send, recv, where):
        return pltpu.make_async_remote_copy(
            src_ref=src, dst_ref=dst, send_sem=send, recv_sem=recv, device_id=where, device_id_type=MESH
        )

    def spread(k):
        def link(m, source, rows_at, where):
            at = wbuf.at[k, source, rows_at]
            return functools.partial(remote, at, at, p_send.at[k, m], p_recv.at[k, m], where)

        everything = slice(0, 2 * part + 8)
        if relay:
            return [
                link(0, dp, everything, (flip, place)),
                link(1, dp, everything, (turn, place)),
                link(2, flip, upper, (turn, place)),
                link(3, turn, lower, (flip, place)),
            ]
        return [link(m - 1, dp, everything, peer(m)) for m in range(1, n_dp)]

    first_hop = 2 if relay else n_dp - 1

    def along(k):
        dz, l = slot(k)
        return remote(pack_ref.at[l], wbuf.at[k, dp], z_send.at[k], z_recv.at[k], plane(nz - dz))

    def own(k):
        dz, l = slot(k)
        return pltpu.make_async_copy(pack_ref.at[l], wbuf.at[k, dp], local_sem.at[4 + 3 * l])

    last = count - 1
    mine = [k for k in range(count) if slot(k)[0] == 0]

    def forward(k):
        if per_device > 1:

            @pl.when(k == last)
            def _():
                own(last).wait()

            @pl.when(k < last)
            def _():
                along(k).wait_recv()
        else:
            along(k).wait_recv()
        for copy in spread(k)[:first_hop]:
            copy().start()

    def pass_on(k):
        if relay:
            hops = spread(k)
            for copy in hops[:first_hop]:
                copy().wait_recv()
            for copy in hops[first_hop:]:
                copy().start()

    def scatter(k):
        def link(m, quarter, at, rows_at, where):
            return functools.partial(
                remote,
                gbuf.at[k, quarter, rows_at],
                rbuf.at[k, at, rows_at],
                a_send.at[k, m],
                a_recv.at[k, m],
                where,
            )

        if relay:
            return [
                link(0, flip, 0, upper, (flip, place)),
                link(1, across, 1, upper, (flip, place)),
                link(2, turn, 0, lower, (turn, place)),
                link(3, across, 1, lower, (turn, place)),
                link(4, turn, 2, upper, (turn, place)),
                link(5, flip, 2, lower, (flip, place)),
            ]
        everything = slice(0, 2 * part + 8)
        return [
            link(m - 1, (dp + m) % n_dp, m - 1, everything, peer(m)) for m in range(1, n_dp)
        ]

    first_sum = 4 if relay else n_dp - 1

    def add_on(k):
        if relay:
            hops = scatter(k)
            hops[1]().wait_recv()
            hops[3]().wait_recv()
            gbuf[k, turn, upper] = gbuf[k, turn, upper] + rbuf[k, 1, upper]
            gbuf[k, flip, lower] = gbuf[k, flip, lower] + rbuf[k, 1, lower]
            hops[4]().start()
            hops[5]().start()

    def deliver(k):
        dz, l = slot(k)
        return remote(psum.at[k], fbuf.at[dz - 1, l], f_send.at[k], f_recv.at[dz - 1, l], plane(dz))

    def collect(k):
        hops = scatter(k)
        for m in [0, 2, 4, 5] if relay else range(n_dp - 1):
            hops[m]().wait_recv()
        total = gbuf[k, dp]
        for m in [0, 2] if relay else range(n_dp - 1):
            total = total + rbuf[k, m]
        psum[k] = total

    own(0).start()
    own(0).wait()
    for copy in spread(0)[:first_hop]:
        copy().start()
    for k in range(1, count):
        if k in mine:
            own(k).start()
        else:
            along(k).start()
    if per_device > 1:
        forward(jnp.int32(last))
    sends = [
        remote(x_hbm, xin.at[1], sib_send.at[0], sib_recv.at[0], sibling),
        remote(cot_hbm, cin.at[1], sib_send.at[1], sib_recv.at[1], sibling),
        remote(grb.at[0], grb.at[1], sib_send.at[2], sib_recv.at[2], sibling),
    ]
    sends[0].start()
    sends[1].start()

    acc[...] = jnp.zeros_like(acc)
    iga[...] = jnp.zeros_like(iga)

    def prepare(half):
        step = 256

        def body(i, _):
            src = pl.ds(pl.multiple_of(i * step, step), step)
            dst = pl.ds(pl.multiple_of(half * rows + i * step, step), step)
            value = xin[half, src, :]
            high, middle, low = split3(value)
            xcat[dst, 0:D] = low
            xcat[dst, D : 2 * D] = middle
            xcat[dst, 2 * D : 3 * D] = high
            high, low = split2(value.T)
            xt[0:D, dst] = high
            xt[D : 2 * D, dst] = low
            for t in range(TASKS):
                value = cin[half, src, t * DOUT : (t + 1) * DOUT]
                high, low = split2(value)
                base = t * 2 * DOUT
                ccat[dst, base : base + DOUT] = low
                ccat[dst, base + DOUT : base + 2 * DOUT] = high
                high, low = split2(value.T)
                ct[base : base + DOUT, dst] = high
                ct[base + DOUT : base + 2 * DOUT, dst] = low
            return 0

        lax.fori_loop(0, rows // step, body, 0)

    def tables(half):
        chosen = grb[half, PAIRS : 2 * PAIRS, :]
        gates = grb[half, 0:PAIRS, :]
        second = lax.broadcasted_iota(jnp.int32, chosen.shape, 0) >= SELECT
        strengths = []
        tasks = []
        for k in range(count):
            hit = chosen == expert_of(k).astype(F32)
            strengths.append(jnp.sum(jnp.where(hit, gates, 0.0), axis=0, keepdims=True))
            tasks.append(jnp.sum(jnp.where(hit & second, 1.0, 0.0), axis=0, keepdims=True))
        strength = jnp.concatenate(strengths, axis=0)
        task = jnp.concatenate(tasks, axis=0)
        st[:, half * rows : (half + 1) * rows] = strength
        mt[:, half * rows : (half + 1) * rows] = task
        table = jnp.concatenate(
            [strength, task, jnp.zeros((lanes - 2 * count, rows), F32)], axis=0
        )
        gm[half * rows : (half + 1) * rows, :] = table.T

    def mm3(left, right_high, right_low):
        high, low = split2(left)
        return (mm(low, right_high) + mm(high, right_low)) + mm(high, right_high)

    sessions = lengths_ref.shape[1]
    spans = lengths_ref[...].astype(F32)
    square = (sessions, sessions)
    wide = jnp.broadcast_to(spans, square)
    line = lax.broadcasted_iota(jnp.int32, square, 0)
    column = lax.broadcasted_iota(jnp.int32, square, 1)
    begin = jnp.sum(jnp.where(column < line, wide, 0.0), axis=1, keepdims=True)
    span = jnp.sum(jnp.where(column == line, wide, 0.0), axis=1, keepdims=True)
    spot = lax.broadcasted_iota(jnp.int32, (sessions, rows), 1).astype(F32)
    member = jnp.where((spot >= begin) & (spot < begin + span), 1.0, 0.0).astype(BF16)
    gates_t = jnp.concatenate(
        [gw_ref[p * kinds + b : p * kinds + b + 1, :] for b in range(kinds) for p in range(PAIRS)], axis=0
    )

    for copy in copies:
        copy.wait()
    prepare(0)
    sums = mm(member, xcat[0:rows, 0:D]) + mm(member, xcat[0:rows, D : 2 * D])
    sums = sums + mm(member, xcat[0:rows, 2 * D : 3 * D])
    means = sums / span
    m_high, m_low = split2(means.T)
    shift = mm3(gates_t, m_high, m_low)
    s_high, s_low = split2(shift)
    logits = mm3(gates_t, xt[0:D, 0:rows], xt[D : 2 * D, 0:rows])
    logits = logits + (mm(s_low, member) + mm(s_high, member))
    chosen = routes_ref[...]
    weight_logit = logits[0:PAIRS]
    group = lax.broadcasted_iota(jnp.int32, (PAIRS, rows), 0) >= SELECT

    def per_task(value, reduce, neutral):
        first = reduce(jnp.where(group, neutral, value), axis=0, keepdims=True)
        second = reduce(jnp.where(group, value, neutral), axis=0, keepdims=True)
        return jnp.where(group, second, first)

    grown = jnp.exp(weight_logit - per_task(weight_logit, jnp.max, -jnp.inf))
    mix = grown / per_task(grown, jnp.sum, 0.0)
    strength = jnp.ones((PAIRS, rows), F32)
    steps, slopes, signs = [], [], []
    for b in range(BITS):
        bit = lax.shift_right_logical(chosen, jnp.full_like(chosen, b)) & 1
        sign = 2.0 * bit.astype(F32) - 1.0
        raw = sign * logits[(b + 1) * PAIRS : (b + 2) * PAIRS] + OFFSET
        c = jnp.clip(raw, -0.5 * SHARPNESS, 0.5 * SHARPNESS)
        steps.append(-2.0 / SHARPNESS**3 * (c * c * c) + 1.5 / SHARPNESS * c + 0.5)
        inside = (raw >= -0.5 * SHARPNESS) & (raw <= 0.5 * SHARPNESS)
        slope = jnp.where(inside, -6.0 / SHARPNESS**3 * (c * c) + 1.5 / SHARPNESS, 0.0)
        slopes.append(sign * slope)
    strength = (steps[0] * steps[1]) * (steps[2] * steps[3])
    grb[0, 0:PAIRS, :] = mix * strength
    grb[0, PAIRS : 2 * PAIRS, :] = chosen.astype(F32)
    sends[2].start()
    saved[0] = mix
    saved[1] = strength
    rest = [
        steps[1] * (steps[2] * steps[3]),
        steps[0] * (steps[2] * steps[3]),
        steps[3] * (steps[0] * steps[1]),
        steps[2] * (steps[0] * steps[1]),
    ]
    for b in range(BITS):
        saved[2 + b] = mix * rest[b] * slopes[b]
    tables(0)
    pass_on(jnp.int32(0))

    def bias_outputs():
        strength = st[...]
        task = mt[...] > 0.5
        total = jnp.zeros((count, DOUT), F32)
        for t in range(TASKS):
            base = t * 2 * DOUT
            total = total + mm3(
                jnp.where(task if t else ~task, strength, 0.0),
                ccat[:, base + DOUT : base + 2 * DOUT],
                ccat[:, base : base + DOUT],
            )
        b2grad[:, 0, :] = total

    lane = lax.broadcasted_iota(jnp.int32, (TILE, lanes), 1)
    tiles = both // TILE

    give_back = [
        remote(acc.at[pl.ds(rows, rows)], ret_out, sib_send.at[3], sib_recv.at[3], sibling),
        remote(iga.at[pl.ds(rows, rows)], ret_ig, sib_send.at[4], sib_recv.at[4], sibling),
        remote(gcp, ret_gc, sib_send.at[5], sib_recv.at[5], sibling),
    ]

    def tile(k, i):
        turned = (i + (k // last) * (tiles // 2)) % tiles
        rs = pl.ds(pl.multiple_of(turned * TILE, TILE), TILE)
        pre = mm(xcat[rs, :], s_w1[...]) + mm(xcat[rs, D : 3 * D], s_w1[0 : 2 * D])
        pre = pre + mm(xcat[rs, 2 * D : 3 * D], s_w1[0:D])
        pre = pre + bias[k, 0:1, :]
        kept = gm[rs, :]
        table = pltpu.roll(kept, (lanes - k) % lanes, 1)
        gate = table[:, 0:1]
        second = table[:, count : count + 1] > 0.5
        picked = jnp.where(second, ccat[rs, 2 * DOUT : 4 * DOUT], ccat[rs, 0 : 2 * DOUT])
        back = mm(picked, s_w2t[...]) + mm(picked[:, DOUT:], s_w2t[0:DOUT])
        hidden = jnp.maximum(pre, 0.0)
        gated = gate * hidden
        inner = jnp.sum(back * hidden, axis=1, keepdims=True)
        gm[rs, :] = jnp.where(lane == 2 * count + k, inner, kept)
        hidden_cot = jnp.where(pre > 0.0, gate * back, 0.0)
        b1acc[...] = b1acc[...] + jnp.sum(hidden_cot.reshape(TILE // 8, 8, HID), axis=0)
        g_high, g_low = split2(gated)
        h_high, h_low = split2(hidden_cot)
        s_gh[rs, 0:HID] = g_high
        s_gh[rs, HID : 2 * HID] = g_low
        s_hc[rs, 0:HID] = h_high
        s_hc[rs, HID : 2 * HID] = h_low
        out = mm(g_low, s_w2[0:HID]) + mm(g_high, s_w2[HID : 2 * HID]) + mm(g_high, s_w2[0:HID])
        out = out + gate * bias[k, 1:2, :]
        acc[rs, 0:DOUT] = acc[rs, 0:DOUT] + jnp.where(second, 0.0, out)
        acc[rs, DOUT : 2 * DOUT] = acc[rs, DOUT : 2 * DOUT] + jnp.where(second, out, 0.0)
        grad = mm(h_low, s_w1t[0:HID]) + mm(h_high, s_w1t[HID : 2 * HID]) + mm(h_high, s_w1t[0:HID])
        iga[rs, :] = iga[rs, :] + grad

    late = [k for k in range(1, count) if k not in mine]
    schedule = [(2 * n, forward, k) for n, k in enumerate(late)]
    if relay:
        schedule += [(0, pass_on, k) for k in mine if k > 0]
        schedule += [(2 * n + 2, pass_on, k) for n, k in enumerate(late)]

    def slot_body(k, _):
        for copy in spread(k)[(first_hop if relay else 0) :]:
            copy().wait_recv()
        w1 = wbuf[k, :, 0:part, :].reshape(D, HID)
        w2 = wbuf[k, :, part : 2 * part, :].reshape(HID, DOUT)
        high, middle, low = split3(w1)
        s_w1[0:D] = high
        s_w1[D : 2 * D] = middle
        s_w1[2 * D : 3 * D] = low
        high, low = split2(w1.T)
        s_w1t[0:HID] = high
        s_w1t[HID : 2 * HID] = low
        high, low = split2(w2)
        s_w2[0:HID] = high
        s_w2[HID : 2 * HID] = low
        high, low = split2(w2.T)
        s_w2t[0:DOUT] = high
        s_w2t[DOUT : 2 * DOUT] = low
        pieces = wbuf[k, 0, 2 * part : 2 * part + 8, :]
        for m in range(1, n_dp):
            pieces = pieces + wbuf[k, m, 2 * part : 2 * part + 8, :]
        bias[k] = pieces
        b1acc[...] = jnp.zeros_like(b1acc)

        def tile_body(i, _):
            for at, action, which in schedule:

                @pl.when(k * tiles + i == at)
                def _(action=action, which=which):
                    action(jnp.int32(which))

            @pl.when((i == tiles // 2) & (k == 0))
            def _():
                for copy in sends:
                    copy.wait_recv()
                prepare(1)
                tables(1)
                bias_outputs()

            if relay:

                @pl.when((i == tiles // 2) & (k >= 1))
                def _():
                    add_on(k - 1)

            @pl.when((i == tiles // 2) & (k == last))
            def _():
                give_back[0].start()
                give_back[1].start()

            tile(k, i)
            return 0

        lax.fori_loop(0, tiles, tile_body, 0)
        h_high, h_low = s_hc[:, 0:HID], s_hc[:, HID : 2 * HID]
        first_grad = mm(xt[0:D], h_low) + mm(xt[D : 2 * D], h_high) + mm(xt[0:D], h_high)
        gbuf[k, :, 0:part, :] = first_grad.reshape(n_dp, part, HID)
        g_high, g_low = s_gh[:, 0:HID], s_gh[:, HID : 2 * HID]
        second = mt[pl.ds(k, 1), :] > 0.5
        c_high = jnp.where(second, ct[2 * DOUT : 3 * DOUT], ct[0:DOUT])
        c_low = jnp.where(second, ct[3 * DOUT : 4 * DOUT], ct[DOUT : 2 * DOUT])
        second_grad = mm(c_high, g_low) + mm(c_low, g_high) + mm(c_high, g_high)
        gbuf[k, :, part : 2 * part, :] = second_grad.T.reshape(n_dp, part, DOUT)
        sums = jnp.concatenate(
            [jnp.sum(b1acc[...], axis=0, keepdims=True), b2grad[k], jnp.zeros((6, HID), F32)], axis=0
        )
        gbuf[k, :, 2 * part : 2 * part + 8, :] = jnp.broadcast_to(sums[None], (n_dp, 8, HID))
        for copy in scatter(k)[:first_sum]:
            copy().start()

        @pl.when(k >= 1)
        def _():
            collect(k - 1)

        @pl.when(k >= 2)
        def _():
            deliver(k - 1).start()

        return 0

    lax.fori_loop(0, count, slot_body, 0)

    inner = gm[...].T[2 * count : 3 * count]
    b2 = bias[:, 1, :]
    task = mt[...] > 0.5
    added = []
    for t in range(TASKS):
        base = t * 2 * DOUT
        added.append(mm3(b2, ct[base : base + DOUT], ct[base + DOUT : base + 2 * DOUT]))
    inner = inner + jnp.where(task, added[1], added[0])

    def pairs_of(half):
        chosen = grb[half, PAIRS : 2 * PAIRS, :]
        total = jnp.zeros((PAIRS, rows), F32)
        for k in range(count):
            hit = chosen == expert_of(k).astype(F32)
            total = total + jnp.where(hit, inner[k : k + 1, half * rows : (half + 1) * rows], 0.0)
        return total

    gcp[...] = pairs_of(1)
    give_back[2].start()
    own_part = pairs_of(0)
    give_back[2].wait_recv()
    gate_cot = own_part + ret_gc[...]
    mix = saved[0]
    pull = gate_cot * saved[1] * mix
    pulls = [pull - mix * per_task(pull, jnp.sum, 0.0)]
    pulls += [gate_cot * saved[2 + b] for b in range(BITS)]
    cots = jnp.concatenate(pulls, axis=0)
    c_high, c_low = split2(cots)
    gathered = lax.dot_general(
        c_low, member, (((1,), (1,)), ((), ())), preferred_element_type=F32
    ) + lax.dot_general(c_high, member, (((1,), (1,)), ((), ())), preferred_element_type=F32)
    m_high, m_low = split2(means)
    x_high, x_low = xcat[0:rows, 2 * D : 3 * D], xcat[0:rows, D : 2 * D]
    ar_own[...] = (
        (mm(c_low, x_high) + mm(c_high, x_low)) + mm(c_high, x_high) + mm3(gathered, m_high, m_low)
    )
    to_sibling = remote(ar_own, ar_sib, r_send.at[0], r_recv.at[0], sibling)
    to_sibling.start()
    add_on(last)

    def to_peer(m):
        return remote(ar_dp.at[dp], ar_dp.at[dp], r_send.at[m], r_recv.at[m], peer(m))

    def to_plane(dz):
        at = n_dp - 1 + dz
        return remote(ar_z.at[z], ar_z.at[z], r_send.at[at], r_recv.at[at], plane(dz))

    level = gathered / jnp.sum(
        jnp.where(column == line, jnp.broadcast_to(span, square), 0.0), axis=0, keepdims=True
    )
    l_high, l_low = split2(level)
    spread_cots = cots + (mm(l_low, member) + mm(l_high, member))
    flat = jnp.concatenate([spread_cots, jnp.zeros((lanes - PAIRS * kinds, rows), F32)], axis=0)
    f_high, f_low = split2(flat.T)
    g_high, g_low = split2(
        jnp.concatenate([gates_t, jnp.zeros((lanes - PAIRS * kinds, D), F32)], axis=0)
    )
    to_sibling.wait_recv()
    ar_dp[dp] = ar_own[...] + ar_sib[...]
    for m in range(1, n_dp):
        to_peer(m).start()
    iga[0:rows, :] = iga[0:rows, :] + (mm(f_low, g_high) + mm(f_high, g_low) + mm(f_high, g_high))
    collect(last)
    if slot(last)[0] != 0:
        deliver(last).start()
    for m in range(1, n_dp):
        to_peer(m).wait_recv()
    total = ar_dp[0]
    for m in range(1, n_dp):
        total = total + ar_dp[m]
    ar_z[z] = total
    for dz in range(1, nz):
        to_plane(dz).start()
    give_back[0].wait_recv()
    give_back[1].wait_recv()

    def finish(i, _):
        rs = pl.ds(pl.multiple_of(i * 256, 256), 256)
        acc[rs, :] = acc[rs, :] + ret_out[rs, :]
        iga[rs, :] = iga[rs, :] + ret_ig[rs, :]
        return 0

    lax.fori_loop(0, rows // 256, finish, 0)
    results = [
        pltpu.make_async_copy(acc.at[pl.ds(0, rows)], out_hbm, local_sem.at[0]),
        pltpu.make_async_copy(iga.at[pl.ds(0, rows)], ig_hbm, local_sem.at[1]),
    ]
    for copy in results:
        copy.start()
    for l in range(per_device):
        total = psum[mine[-1 - l] if per_device == 1 else [k for k in mine if slot(k)[1] == l][0]]
        for dz in range(1, nz):
            remote(
                psum.at[0], fbuf.at[dz - 1, l], f_send.at[0], f_recv.at[dz - 1, l], plane(dz)
            ).wait_recv()
            total = total + fbuf[dz - 1, l]
        gsum_ref[l] = total
    for dz in range(1, nz):
        to_plane(dz).wait_recv()
    total = ar_z[0]
    for dz in range(1, nz):
        total = total + ar_z[dz]
    gg_ref[...] = jnp.concatenate(
        [total[b * PAIRS + p : b * PAIRS + p + 1] for p in range(PAIRS) for b in range(kinds)], axis=0
    )
    for copy in results:
        copy.wait()

    for copy in sends + give_back + [to_sibling]:
        copy.wait_send()
    for m in range(1, n_dp):
        to_peer(m).wait_send()
    for dz in range(1, nz):
        to_plane(dz).wait_send()

    def drain(k, _):
        for copy in spread(k) + scatter(k):
            copy().wait_send()
        return 0

    lax.fori_loop(0, count, drain, 0)
    own_last = [k for k in mine if k > 0]

    def drain_z(k, _):
        along(k).wait_send()
        deliver(k).wait_send()
        return 0

    lax.fori_loop(1, count - len(own_last), drain_z, 0)


def run_experts(features, cotangent, routes_t, lengths, gates_t, first_weight, second_weight, expert_bias):
    rows = features.shape[0]
    n_dp, n_expert = lax.axis_size("dp"), lax.axis_size("expert")
    nz = n_expert // CORES
    per_device, part, _ = first_weight.shape
    height = 2 * part + 8
    count = nz * per_device
    both = CORES * rows
    heads = PAIRS * (BITS + 1)
    hops = n_dp - 1
    gather_hops, sum_hops = (4, 6) if n_dp == 4 else (hops, hops)
    any_spec = pl.BlockSpec(memory_space=pl.ANY)
    vmem = pl.BlockSpec(memory_space=pltpu.VMEM)
    dma = pltpu.SemaphoreType.DMA
    return pl.pallas_call(
        functools.partial(expert_kernel, (rows, n_dp, nz, per_device)),
        out_shape=(
            jax.ShapeDtypeStruct((rows, TASKS * DOUT), F32),
            jax.ShapeDtypeStruct((rows, D), F32),
            jax.ShapeDtypeStruct((per_device, height, D), F32),
            jax.ShapeDtypeStruct((heads, D), F32),
        ),
        in_specs=[any_spec, any_spec, vmem, vmem, vmem, any_spec, any_spec, vmem],
        out_specs=(any_spec, any_spec, vmem, vmem),
        scratch_shapes=[
            pltpu.VMEM((per_device, height, D), F32),
            pltpu.VMEM((2, rows, D), F32),
            pltpu.VMEM((2, rows, TASKS * DOUT), F32),
            pltpu.VMEM((2, 2 * PAIRS, rows), F32),
            pltpu.VMEM((both, 3 * D), BF16),
            pltpu.VMEM((2 * D, both), BF16),
            pltpu.VMEM((both, 4 * DOUT), BF16),
            pltpu.VMEM((4 * DOUT, both), BF16),
            pltpu.VMEM((both, 128), F32),
            pltpu.VMEM((count, both), F32),
            pltpu.VMEM((count, both), F32),
            pltpu.VMEM((both, TASKS * DOUT), F32),
            pltpu.VMEM((both, D), F32),
            pltpu.VMEM((both, 2 * HID), BF16),
            pltpu.VMEM((both, 2 * HID), BF16),
            pltpu.VMEM((3 * D, HID), BF16),
            pltpu.VMEM((2 * HID, D), BF16),
            pltpu.VMEM((2 * HID, DOUT), BF16),
            pltpu.VMEM((2 * DOUT, HID), BF16),
            pltpu.VMEM((count, 8, HID), F32),
            pltpu.VMEM((8, HID), F32),
            pltpu.VMEM((count, 1, DOUT), F32),
            pltpu.VMEM((count, n_dp, height, D), F32),
            pltpu.VMEM((count, n_dp, height, D), F32),
            pltpu.VMEM((count, hops, height, D), F32),
            pltpu.VMEM((count, height, D), F32),
            pltpu.VMEM((nz - 1, per_device, height, D), F32),
            pltpu.VMEM((rows, TASKS * DOUT), F32),
            pltpu.VMEM((rows, D), F32),
            pltpu.VMEM((PAIRS, rows), F32),
            pltpu.VMEM((PAIRS, rows), F32),
            pltpu.VMEM((2 + BITS, PAIRS, rows), F32),
            pltpu.VMEM((heads, D), F32),
            pltpu.VMEM((heads, D), F32),
            pltpu.VMEM((n_dp, heads, D), F32),
            pltpu.VMEM((nz, heads, D), F32),
            dma((2 + 3 * per_device,)),
            dma((6,)),
            dma((6,)),
            dma((count,)),
            dma((count,)),
            dma((count, gather_hops)),
            dma((count, gather_hops)),
            dma((count, sum_hops)),
            dma((count, sum_hops)),
            dma((count,)),
            dma((nz - 1, per_device)),
            dma((n_dp + nz - 1,)),
            dma((n_dp + nz - 1,)),
        ],
        compiler_params=pltpu.CompilerParams(
            collective_id=0, has_side_effects=True, vmem_limit_bytes=60 << 20
        ),
    )(features, cotangent, routes_t, lengths, gates_t, first_weight, second_weight, expert_bias)


def update_kernel(scale, out_raw, ig_raw, gsum, gg, *refs):
    weights, outs = refs[:12], refs[14:26]
    out_ref, ig_ref = refs[12:14]
    out_held, ig_held, load_sem, store_sem = refs[26:]
    loads, stores = [], []
    for n, (src, held, dst) in enumerate([(out_raw, out_held, out_ref), (ig_raw, ig_held, ig_ref)]):
        step = src.shape[0] // PIECES
        for i in range(PIECES):
            rs = pl.ds(i * step, step)
            loads.append(pltpu.make_async_copy(src.at[rs], held.at[rs], load_sem.at[n, i]))
            stores.append(pltpu.make_async_copy(held.at[rs], dst.at[rs], store_sem.at[n, i]))
    for copy in loads:
        copy.start()
    per_device, part, _ = weights[3].shape
    width = weights[9].shape[1]
    dp = lax.axis_index("dp")
    bias_grad = []
    for l in range(per_device):
        mine = jnp.zeros((1, width), F32)
        for q in range(2 * HID // width):
            row, lane = q * width // HID, q * width % HID
            mine = jnp.where(dp == q, gsum[l, 2 * part + row : 2 * part + row + 1, lane : lane + width], mine)
        bias_grad.append(mine)
    grads = [
        (gg[...], GATE_RATE),
        (gsum[:, 0:part], EXPERT_RATE),
        (gsum[:, part : 2 * part], EXPERT_RATE),
        (jnp.concatenate(bias_grad, axis=0), EXPERT_RATE),
    ]
    for n, (gradient, rate) in enumerate(grads):
        weight, momentum, average = weights[3 * n : 3 * n + 3]
        news = update(weight[...], gradient * scale, momentum[...], average[...], rate)
        for ref, value in zip(outs[3 * n : 3 * n + 3], news):
            ref[...] = value
    for load, store in zip(loads, stores):
        load.wait()
        store.start()
    for copy in stores:
        copy.wait()


def run_updates(scale, out_raw, ig_raw, gsum, gg, weights):
    any_spec = pl.BlockSpec(memory_space=pl.ANY)
    vmem = pl.BlockSpec(memory_space=pltpu.VMEM)
    shapes = [out_raw, ig_raw] + [weights[3 * (n // 3)] for n in range(12)]
    return pl.pallas_call(
        functools.partial(update_kernel, scale),
        out_shape=tuple(jax.ShapeDtypeStruct(array.shape, F32) for array in shapes),
        in_specs=[any_spec, any_spec] + [vmem] * 14,
        out_specs=(any_spec, any_spec) + (vmem,) * 12,
        scratch_shapes=[
            pltpu.VMEM(out_raw.shape, F32),
            pltpu.VMEM(ig_raw.shape, F32),
            pltpu.SemaphoreType.DMA((2, PIECES)),
            pltpu.SemaphoreType.DMA((2, PIECES)),
        ],
    )(out_raw, ig_raw, gsum, gg, *weights)


def local(
    features,
    cotangent,
    routes,
    lengths,
    gate_weight,
    first_weight,
    second_weight,
    expert_bias,
    gate_momentum,
    gate_average,
    first_momentum,
    first_average,
    second_momentum,
    second_average,
    bias_momentum,
    bias_average,
):
    out_raw, ig_raw, gsum, gg = run_experts(
        features, cotangent, routes.T, lengths, gate_weight.T, first_weight, second_weight, expert_bias
    )
    row_count = features.shape[0] * lax.axis_size("dp") * lax.axis_size("expert")
    results = run_updates(
        1.0 / math.sqrt(row_count),
        out_raw,
        ig_raw,
        gsum,
        gg,
        [
            gate_weight.T,
            gate_momentum.T,
            gate_average.T,
            first_weight,
            first_momentum,
            first_average,
            second_weight,
            second_momentum,
            second_average,
            expert_bias,
            bias_momentum,
            bias_average,
        ],
    )
    return (*results[:2], *(value.T for value in results[2:5]), *results[5:])


def solution(mesh):
    rows = P(("dp", "expert"), None)
    weight = P("expert", "dp", None)
    bias = P("expert", "dp")
    return jax.shard_map(
        local,
        mesh=mesh,
        in_specs=(
            rows,
            rows,
            rows,
            rows,
            P(),
            weight,
            weight,
            bias,
            P(),
            P(),
            weight,
            weight,
            weight,
            weight,
            bias,
            bias,
        ),
        out_specs=(
            rows,
            rows,
            P(),
            P(),
            P(),
            weight,
            weight,
            weight,
            weight,
            weight,
            weight,
            bias,
            bias,
            bias,
        ),
        check_vma=False,
    )
```

```python
import functools
import math

import jax
import jax.numpy as jnp
from jax import lax
from jax.experimental import pallas as pl
from jax.experimental.pallas import tpu as pltpu
from jax.sharding import PartitionSpec as P

D = 256
HID = 256
DOUT = 256
EXPERTS = 16
BITS = 4
TASKS = 2
SELECT = 4
PAIRS = TASKS * SELECT
CORES = 2
PIECES = 4

OFFSET = 3.5
SHARPNESS = 10.0
MOMENTUM = 0.5
AVERAGE_DECAY = 0.5
EXPERT_RATE = 0.4
GATE_RATE = 0.01
F32 = jnp.float32
BF16 = jnp.bfloat16
MESH = pl.DeviceIdType.MESH


def update(weight, gradient, momentum, average, step_rate):
    momentum_new = MOMENTUM * momentum + gradient
    weight_new = weight - step_rate * (gradient + MOMENTUM * momentum_new)
    average_new = AVERAGE_DECAY * average + (1.0 - AVERAGE_DECAY) * weight_new
    return (momentum_new, weight_new, average_new)


def mm(left, right):
    return jnp.dot(left, right, preferred_element_type=F32)


def split2(value):
    high = value.astype(BF16)
    return high, (value - high.astype(F32)).astype(BF16)


def split3(value):
    high = value.astype(BF16)
    rest = value - high.astype(F32)
    middle = rest.astype(BF16)
    return high, middle, (rest - middle.astype(F32)).astype(BF16)


def expert_kernel(
    dims,
    x_hbm,
    cot_hbm,
    routes_ref,
    lengths_ref,
    gw_ref,
    first_hbm,
    second_hbm,
    bias_ref,
    out_hbm,
    ig_hbm,
    gsum_ref,
    gg_ref,
    pack_ref,
    xin,
    cin,
    grb,
    xcat,
    xt,
    ccat,
    ct,
    gm,
    st,
    mt,
    acc,
    iga,
    s_gh,
    s_hc,
    s_w1,
    s_w1t,
    s_w2,
    s_w2t,
    bias,
    b1acc,
    b2grad,
    wbuf,
    rbuf,
    psum,
    fbuf,
    ret_gc,
    gcp,
    saved,
    ar_own,
    ar_sib,
    ar_dp,
    ar_z,
    local_sem,
    sib_send,
    sib_recv,
    z_send,
    z_recv,
    p_send,
    p_recv,
    a_send,
    a_recv,
    f_send,
    f_recv,
    r_send,
    r_recv,
    free_sem,
):
    rows, n_dp, nz, per_device = dims
    count = nz * per_device
    part = D // n_dp
    lanes = 128
    kinds = BITS + 1
    both = CORES * rows
    relay = n_dp == 4
    tile_rows = rows
    width = 2 * HID // n_dp
    upper, lower, everything = slice(0, part), slice(part, 2 * part + 8), slice(0, 2 * part + 8)
    dp = lax.axis_index("dp")
    place = lax.axis_index("expert")
    z = place // CORES
    core = place % CORES
    sibling = (dp, z * CORES + (1 - core))

    def peer(m):
        return ((dp + m) % n_dp, place)

    def plane_at(step):
        total, bit = 0, 1
        while bit < nz:
            here, there = (z // bit) % 2, (step // bit) % 2
            total = total + bit * (here + there - 2 * here * there)
            bit *= 2
        return total

    def plane(step):
        return (dp, plane_at(step) * CORES + core)

    flip = (dp // 2) * 2 + (1 - dp % 2)
    turn = (1 - dp // 2) * 2 + dp % 2
    across = (n_dp - 1) - dp

    def slot(k):
        turn_of = k + (per_device - 1)
        step = (turn_of // per_device) % nz
        return step, turn_of % per_device

    def expert_of(k):
        dz, l = slot(k)
        return (plane_at(dz) * CORES + core) * per_device + l

    barrier = pltpu.get_barrier_semaphore()
    greet = [sibling] + [peer(m) for m in range(1, n_dp)] + [plane(dz) for dz in range(1, nz)]
    for other in greet:
        pl.semaphore_signal(barrier, inc=1, device_id=other, device_id_type=MESH)
    copies = [
        pltpu.make_async_copy(x_hbm, xin.at[0], local_sem.at[0]),
        pltpu.make_async_copy(cot_hbm, cin.at[0], local_sem.at[1]),
    ]
    loads = []
    for l in range(per_device):
        loads += [
            pltpu.make_async_copy(first_hbm.at[l], pack_ref.at[l, upper], local_sem.at[2 + 3 * l]),
            pltpu.make_async_copy(
                second_hbm.at[l], pack_ref.at[l, slice(part, 2 * part)], local_sem.at[3 + 3 * l]
            ),
        ]
    for copy in loads + copies:
        copy.start()
    spread_lane = lax.broadcasted_iota(jnp.int32, (1, HID), 1)
    bias_row, bias_lane = dp * width // HID, dp * width % HID
    for l in range(per_device):
        wide = jnp.concatenate([bias_ref[l : l + 1, :]] * (HID // width), axis=1)
        wide = jnp.where((spread_lane >= bias_lane) & (spread_lane < bias_lane + width), wide, 0.0)
        rows_of = lax.broadcasted_iota(jnp.int32, (8, HID), 0)
        pack_ref[l, 2 * part : 2 * part + 8, :] = jnp.where(rows_of == bias_row, wide, 0.0)
    for copy in loads:
        copy.wait()
    pl.semaphore_wait(barrier, len(greet))

    def remote(src, dst, send, recv, where):
        return pltpu.make_async_remote_copy(
            src_ref=src, dst_ref=dst, send_sem=send, recv_sem=recv, device_id=where, device_id_type=MESH
        )

    def spread(k):
        def link(m, source, rows_at, where):
            at = wbuf.at[k, source, rows_at]
            return functools.partial(remote, at, at, p_send.at[k, m], p_recv.at[k, m], where)

        if relay:
            return [
                link(0, dp, everything, (flip, place)),
                link(1, dp, everything, (turn, place)),
                link(2, flip, upper, (turn, place)),
                link(3, turn, lower, (flip, place)),
            ]
        return [link(m - 1, dp, everything, peer(m)) for m in range(1, n_dp)]

    first_hop = 2 if relay else n_dp - 1

    def along(k):
        dz, l = slot(k)
        return remote(
            pack_ref.at[l, everything], wbuf.at[k, dp, everything], z_send.at[k], z_recv.at[k], plane(dz)
        )

    def assembled(k):
        for copy in spread(k)[(first_hop if relay else 0) :]:
            copy().wait_recv()

    def own(k):
        dz, l = slot(k)
        return pltpu.make_async_copy(pack_ref.at[l], wbuf.at[k, dp], local_sem.at[4 + 3 * l])

    last = count - 1
    mine = [k for k in range(count) if slot(k)[0] == 0]

    def forward(k):
        if per_device > 1:

            @pl.when(k == last)
            def _():
                own(last).wait()

            @pl.when(k < last)
            def _():
                along(k).wait_recv()
        else:
            along(k).wait_recv()
        for copy in spread(k)[:first_hop]:
            copy().start()

    def pass_on(k):
        if relay:
            hops = spread(k)
            for copy in hops[:first_hop]:
                copy().wait_recv()
            for copy in hops[first_hop:]:
                copy().start()

    def scatter(k):
        def link(m, quarter, at, rows_at, where):
            return functools.partial(
                remote,
                wbuf.at[k, quarter, rows_at],
                rbuf.at[k, at, rows_at],
                a_send.at[k, m],
                a_recv.at[k, m],
                where,
            )

        if relay:
            return [
                link(0, flip, 0, upper, (flip, place)),
                link(1, across, 1, upper, (flip, place)),
                link(2, turn, 0, lower, (turn, place)),
                link(3, across, 1, lower, (turn, place)),
                link(4, turn, 2, upper, (turn, place)),
                link(5, flip, 2, lower, (flip, place)),
            ]
        return [
            link(m - 1, (dp + m) % n_dp, m - 1, everything, peer(m)) for m in range(1, n_dp)
        ]

    first_sum = 4 if relay else n_dp - 1

    def add_on(k):
        if relay:
            hops = scatter(k)
            hops[1]().wait_recv()
            hops[3]().wait_recv()
            wbuf[k, turn, upper] = wbuf[k, turn, upper] + rbuf[k, 1, upper]
            wbuf[k, flip, lower] = wbuf[k, flip, lower] + rbuf[k, 1, lower]
            hops[4]().start()
            hops[5]().start()

    def deliver(k):
        dz, l = slot(k)
        return remote(
            psum.at[k, everything],
            fbuf.at[dz - 1, l, everything],
            f_send.at[k],
            f_recv.at[dz - 1, l],
            plane(dz),
        )

    def collect(k):
        hops = scatter(k)
        for m in [0, 2, 4, 5] if relay else range(n_dp - 1):
            hops[m]().wait_recv()
        total = wbuf[k, dp]
        for m in [0, 2] if relay else range(n_dp - 1):
            total = total + rbuf[k, m]
        psum[k] = total

    own(0).start()
    own(0).wait()
    for copy in spread(0)[:first_hop]:
        copy().start()
    for k in mine[1:]:
        own(k).start()
    late = [k for k in range(1, count) if k not in mine]

    def send_along(k):
        along(k).start()

    send_along(late[0])
    sends = [
        remote(x_hbm, xin.at[1], sib_send.at[0], sib_recv.at[0], sibling),
        remote(cot_hbm, cin.at[1], sib_send.at[1], sib_recv.at[1], sibling),
        remote(grb.at[0], grb.at[1], sib_send.at[2], sib_recv.at[2], sibling),
    ]
    sends[0].start()
    sends[1].start()

    acc[...] = jnp.zeros_like(acc)
    iga[...] = jnp.zeros_like(iga)

    def prepare(half):
        step = 256

        def body(i, _):
            src = pl.ds(pl.multiple_of(i * step, step), step)
            dst = pl.ds(pl.multiple_of(half * rows + i * step, step), step)
            value = xin[half, src, :]
            high, middle, low = split3(value)
            xcat[dst, 0:D] = low
            xcat[dst, D : 2 * D] = middle
            xcat[dst, 2 * D : 3 * D] = high
            high, low = split2(value.T)
            xt[0:D, dst] = high
            xt[D : 2 * D, dst] = low
            for t in range(TASKS):
                value = cin[half, src, t * DOUT : (t + 1) * DOUT]
                high, low = split2(value)
                base = t * 2 * DOUT
                ccat[dst, base : base + DOUT] = low
                ccat[dst, base + DOUT : base + 2 * DOUT] = high
                high, low = split2(value.T)
                ct[base : base + DOUT, dst] = high
                ct[base + DOUT : base + 2 * DOUT, dst] = low
            return 0

        lax.fori_loop(0, rows // step, body, 0)

    def tables(half):
        chosen = grb[half, PAIRS : 2 * PAIRS, :]
        gates = grb[half, 0:PAIRS, :]
        second = lax.broadcasted_iota(jnp.int32, chosen.shape, 0) >= SELECT
        strengths = []
        tasks = []
        for k in range(count):
            hit = chosen == expert_of(k).astype(F32)
            strengths.append(jnp.sum(jnp.where(hit, gates, 0.0), axis=0, keepdims=True))
            tasks.append(jnp.sum(jnp.where(hit & second, 1.0, 0.0), axis=0, keepdims=True))
        strength = jnp.concatenate(strengths, axis=0)
        task = jnp.concatenate(tasks, axis=0)
        st[:, half * rows : (half + 1) * rows] = strength
        mt[:, half * rows : (half + 1) * rows] = task
        table = jnp.concatenate(
            [strength, task, jnp.zeros((lanes - 2 * count, rows), F32)], axis=0
        )
        gm[half * rows : (half + 1) * rows, :] = table.T

    def mm3(left, right_high, right_low):
        high, low = split2(left)
        return (mm(low, right_high) + mm(high, right_low)) + mm(high, right_high)

    sessions = lengths_ref.shape[1]
    spans = lengths_ref[...].astype(F32)
    square = (sessions, sessions)
    wide = jnp.broadcast_to(spans, square)
    line = lax.broadcasted_iota(jnp.int32, square, 0)
    column = lax.broadcasted_iota(jnp.int32, square, 1)
    begin = jnp.sum(jnp.where(column < line, wide, 0.0), axis=1, keepdims=True)
    span = jnp.sum(jnp.where(column == line, wide, 0.0), axis=1, keepdims=True)
    spot = lax.broadcasted_iota(jnp.int32, (sessions, rows), 1).astype(F32)
    member = jnp.where((spot >= begin) & (spot < begin + span), 1.0, 0.0).astype(BF16)
    gates_t = jnp.concatenate(
        [gw_ref[p * kinds + b : p * kinds + b + 1, :] for b in range(kinds) for p in range(PAIRS)], axis=0
    )

    for copy in copies:
        copy.wait()
    prepare(0)
    send_along(late[1])
    sums = mm(member, xcat[0:rows, 0:D]) + mm(member, xcat[0:rows, D : 2 * D])
    sums = sums + mm(member, xcat[0:rows, 2 * D : 3 * D])
    means = sums / span
    m_high, m_low = split2(means.T)
    shift = mm3(gates_t, m_high, m_low)
    s_high, s_low = split2(shift)
    logits = mm3(gates_t, xt[0:D, 0:rows], xt[D : 2 * D, 0:rows])
    logits = logits + (mm(s_low, member) + mm(s_high, member))
    chosen = routes_ref[...]
    weight_logit = logits[0:PAIRS]
    group = lax.broadcasted_iota(jnp.int32, (PAIRS, rows), 0) >= SELECT

    def per_task(value, reduce, neutral):
        first = reduce(jnp.where(group, neutral, value), axis=0, keepdims=True)
        second = reduce(jnp.where(group, value, neutral), axis=0, keepdims=True)
        return jnp.where(group, second, first)

    grown = jnp.exp(weight_logit - per_task(weight_logit, jnp.max, -jnp.inf))
    mix = grown / per_task(grown, jnp.sum, 0.0)
    strength = jnp.ones((PAIRS, rows), F32)
    steps, slopes, signs = [], [], []
    for b in range(BITS):
        bit = lax.shift_right_logical(chosen, jnp.full_like(chosen, b)) & 1
        sign = 2.0 * bit.astype(F32) - 1.0
        raw = sign * logits[(b + 1) * PAIRS : (b + 2) * PAIRS] + OFFSET
        c = jnp.clip(raw, -0.5 * SHARPNESS, 0.5 * SHARPNESS)
        steps.append(-2.0 / SHARPNESS**3 * (c * c * c) + 1.5 / SHARPNESS * c + 0.5)
        inside = (raw >= -0.5 * SHARPNESS) & (raw <= 0.5 * SHARPNESS)
        slope = jnp.where(inside, -6.0 / SHARPNESS**3 * (c * c) + 1.5 / SHARPNESS, 0.0)
        slopes.append(sign * slope)
    strength = (steps[0] * steps[1]) * (steps[2] * steps[3])
    grb[0, 0:PAIRS, :] = mix * strength
    grb[0, PAIRS : 2 * PAIRS, :] = chosen.astype(F32)
    sends[2].start()
    saved[0] = mix
    saved[1] = strength
    rest = [
        steps[1] * (steps[2] * steps[3]),
        steps[0] * (steps[2] * steps[3]),
        steps[3] * (steps[0] * steps[1]),
        steps[2] * (steps[0] * steps[1]),
    ]
    for b in range(BITS):
        saved[2 + b] = mix * rest[b] * slopes[b]
    tables(0)
    pass_on(jnp.int32(0))
    forward(jnp.int32(1))
    send_along(late[2])

    def bias_outputs():
        strength = st[...]
        task = mt[...] > 0.5
        total = jnp.zeros((count, DOUT), F32)
        for t in range(TASKS):
            base = t * 2 * DOUT
            total = total + mm3(
                jnp.where(task if t else ~task, strength, 0.0),
                ccat[:, base + DOUT : base + 2 * DOUT],
                ccat[:, base : base + DOUT],
            )
        b2grad[:, 0, :] = total

    lane = lax.broadcasted_iota(jnp.int32, (tile_rows, lanes), 1)
    tiles = both // tile_rows

    give_back = [
        remote(acc.at[pl.ds(rows, rows)], cin.at[1], sib_send.at[3], sib_recv.at[3], sibling),
        remote(iga.at[pl.ds(rows, rows)], xin.at[1], sib_send.at[4], sib_recv.at[4], sibling),
        remote(gcp, ret_gc, sib_send.at[5], sib_recv.at[5], sibling),
    ]

    def tile(k, i):
        turned = (i + (k // last) * (tiles // 2)) % tiles
        rs = pl.ds(pl.multiple_of(turned * tile_rows, tile_rows), tile_rows)
        pre = mm(xcat[rs, :], s_w1[...]) + mm(xcat[rs, D : 3 * D], s_w1[0 : 2 * D])
        pre = pre + mm(xcat[rs, 2 * D : 3 * D], s_w1[0:D])
        pre = pre + bias[k, 0:1, :]
        kept = gm[rs, :]
        table = pltpu.roll(kept, (lanes - k) % lanes, 1)
        gate = table[:, 0:1]
        second = table[:, count : count + 1] > 0.5
        picked = jnp.where(second, ccat[rs, 2 * DOUT : 4 * DOUT], ccat[rs, 0 : 2 * DOUT])
        back = mm(picked, s_w2t[...]) + mm(picked[:, DOUT:], s_w2t[0:DOUT])
        hidden = jnp.maximum(pre, 0.0)
        gated = gate * hidden
        inner = jnp.sum(back * hidden, axis=1, keepdims=True)
        gm[rs, :] = jnp.where(lane == 2 * count + k, inner, kept)
        hidden_cot = jnp.where(pre > 0.0, gate * back, 0.0)
        b1acc[...] = b1acc[...] + jnp.sum(hidden_cot.reshape(tile_rows // 8, 8, HID), axis=0)
        g_high, g_low = split2(gated)
        h_high, h_low = split2(hidden_cot)
        s_gh[rs, 0:HID] = g_high
        s_gh[rs, HID : 2 * HID] = g_low
        s_hc[rs, 0:HID] = h_high
        s_hc[rs, HID : 2 * HID] = h_low
        out = mm(g_low, s_w2[0:HID]) + mm(g_high, s_w2[HID : 2 * HID]) + mm(g_high, s_w2[0:HID])
        out = out + gate * bias[k, 1:2, :]
        acc[rs, 0:DOUT] = acc[rs, 0:DOUT] + jnp.where(second, 0.0, out)
        acc[rs, DOUT : 2 * DOUT] = acc[rs, DOUT : 2 * DOUT] + jnp.where(second, out, 0.0)
        grad = mm(h_low, s_w1t[0:HID]) + mm(h_high, s_w1t[HID : 2 * HID]) + mm(h_high, s_w1t[0:HID])
        iga[rs, :] = iga[rs, :] + grad

    def settle(k):
        collect(k)

        @pl.when(k >= 1)
        def _():
            deliver(k).start()

    def slot_body(k, _):
        assembled(k)

        @pl.when((k >= 1) & (k + 1 < count))
        def _():
            pass_on(k + 1)

        @pl.when(k + 4 <= late[-1])
        def _():
            send_along(k + 4)

        w1 = wbuf[k, :, 0:part, :].reshape(D, HID)
        w2 = wbuf[k, :, part : 2 * part, :].reshape(HID, DOUT)
        high, middle, low = split3(w1)
        s_w1[0:D] = high
        s_w1[D : 2 * D] = middle
        s_w1[2 * D : 3 * D] = low
        high, low = split2(w1.T)
        s_w1t[0:HID] = high
        s_w1t[HID : 2 * HID] = low
        high, low = split2(w2)
        s_w2[0:HID] = high
        s_w2[HID : 2 * HID] = low
        high, low = split2(w2.T)
        s_w2t[0:DOUT] = high
        s_w2t[DOUT : 2 * DOUT] = low
        pieces = wbuf[k, 0, 2 * part : 2 * part + 2, :]
        for m in range(1, n_dp):
            pieces = pieces + wbuf[k, m, 2 * part : 2 * part + 2, :]
        bias[k, 0:2] = pieces
        b1acc[...] = jnp.zeros_like(b1acc)

        def tile_body(i, _):
            @pl.when(i == tiles // 2)
            def _():
                @pl.when(k == 0)
                def _():
                    for copy in sends:
                        copy.wait_recv()
                    prepare(1)
                    pl.semaphore_signal(free_sem, inc=1, device_id=sibling, device_id_type=MESH)
                    tables(1)
                    bias_outputs()
                    pass_on(jnp.int32(1))
                    forward(jnp.int32(2))
                    forward(jnp.int32(3))

                @pl.when((k >= 1) & (k + 3 < count))
                def _():
                    forward(k + 3)

                @pl.when(k == last)
                def _():
                    pl.semaphore_wait(free_sem, 1)
                    give_back[0].start()
                    give_back[1].start()

                @pl.when(k >= 2)
                def _():
                    settle(k - 2)

            tile(k, i)
            return 0

        lax.fori_loop(0, tiles, tile_body, 0)

        @pl.when(k >= 1)
        def _():
            add_on(k - 1)

        for copy in spread(k):
            copy().wait_send()
        h_high, h_low = s_hc[:, 0:HID], s_hc[:, HID : 2 * HID]
        first_grad = mm(xt[0:D], h_low) + mm(xt[D : 2 * D], h_high) + mm(xt[0:D], h_high)
        wbuf[k, :, 0:part, :] = first_grad.reshape(n_dp, part, HID)
        g_high, g_low = s_gh[:, 0:HID], s_gh[:, HID : 2 * HID]
        second = mt[pl.ds(k, 1), :] > 0.5
        c_high = jnp.where(second, ct[2 * DOUT : 3 * DOUT], ct[0:DOUT])
        c_low = jnp.where(second, ct[3 * DOUT : 4 * DOUT], ct[DOUT : 2 * DOUT])
        second_grad = mm(c_high, g_low) + mm(c_low, g_high) + mm(c_high, g_high)
        wbuf[k, :, part : 2 * part, :] = second_grad.T.reshape(n_dp, part, DOUT)
        sums = jnp.concatenate(
            [jnp.sum(b1acc[...], axis=0, keepdims=True), b2grad[k], jnp.zeros((6, HID), F32)], axis=0
        )
        wbuf[k, :, 2 * part : 2 * part + 8, :] = jnp.broadcast_to(sums[None], (n_dp, 8, HID))
        for copy in scatter(k)[:first_sum]:
            copy().start()

        @pl.when(k == last)
        def _():
            settle(k - 1)

        return 0

    lax.fori_loop(0, count, slot_body, 0)

    inner = gm[...].T[2 * count : 3 * count]
    b2 = bias[:, 1, :]
    task = mt[...] > 0.5
    added = []
    for t in range(TASKS):
        base = t * 2 * DOUT
        added.append(mm3(b2, ct[base : base + DOUT], ct[base + DOUT : base + 2 * DOUT]))
    inner = inner + jnp.where(task, added[1], added[0])

    def pairs_of(half):
        chosen = grb[half, PAIRS : 2 * PAIRS, :]
        total = jnp.zeros((PAIRS, rows), F32)
        for k in range(count):
            hit = chosen == expert_of(k).astype(F32)
            total = total + jnp.where(hit, inner[k : k + 1, half * rows : (half + 1) * rows], 0.0)
        return total

    gcp[...] = pairs_of(1)
    give_back[2].start()
    own_part = pairs_of(0)
    give_back[0].wait_recv()

    def finish_out(i, _):
        rs = pl.ds(pl.multiple_of(i * 256, 256), 256)
        acc[rs, :] = acc[rs, :] + cin[1, rs, :]
        return 0

    lax.fori_loop(0, rows // 256, finish_out, 0)
    results = [
        pltpu.make_async_copy(acc.at[pl.ds(0, rows)], out_hbm, local_sem.at[0]),
        pltpu.make_async_copy(iga.at[pl.ds(0, rows)], ig_hbm, local_sem.at[1]),
    ]
    results[0].start()
    give_back[2].wait_recv()
    gate_cot = own_part + ret_gc[...]
    mix = saved[0]
    pull = gate_cot * saved[1] * mix
    pulls = [pull - mix * per_task(pull, jnp.sum, 0.0)]
    pulls += [gate_cot * saved[2 + b] for b in range(BITS)]
    cots = jnp.concatenate(pulls, axis=0)
    c_high, c_low = split2(cots)
    gathered = lax.dot_general(
        c_low, member, (((1,), (1,)), ((), ())), preferred_element_type=F32
    ) + lax.dot_general(c_high, member, (((1,), (1,)), ((), ())), preferred_element_type=F32)
    m_high, m_low = split2(means)
    x_high, x_low = xcat[0:rows, 2 * D : 3 * D], xcat[0:rows, D : 2 * D]
    ar_own[...] = (
        (mm(c_low, x_high) + mm(c_high, x_low)) + mm(c_high, x_high) + mm3(gathered, m_high, m_low)
    )
    to_sibling = remote(ar_own, ar_sib, r_send.at[0], r_recv.at[0], sibling)
    to_sibling.start()
    add_on(last)

    def to_peer(m):
        return remote(ar_dp.at[dp], ar_dp.at[dp], r_send.at[m], r_recv.at[m], peer(m))

    def to_plane(dz):
        at = n_dp - 1 + dz
        return remote(ar_z.at[z], ar_z.at[z], r_send.at[at], r_recv.at[at], plane(dz))

    level = gathered / jnp.sum(
        jnp.where(column == line, jnp.broadcast_to(span, square), 0.0), axis=0, keepdims=True
    )
    l_high, l_low = split2(level)
    spread_cots = cots + (mm(l_low, member) + mm(l_high, member))
    flat = jnp.concatenate([spread_cots, jnp.zeros((lanes - PAIRS * kinds, rows), F32)], axis=0)
    f_high, f_low = split2(flat.T)
    g_high, g_low = split2(
        jnp.concatenate([gates_t, jnp.zeros((lanes - PAIRS * kinds, D), F32)], axis=0)
    )
    to_sibling.wait_recv()
    ar_dp[dp] = ar_own[...] + ar_sib[...]
    for m in range(1, n_dp):
        to_peer(m).start()
    give_back[1].wait_recv()
    from_gate = mm(f_low, g_high) + mm(f_high, g_low) + mm(f_high, g_high)
    iga[0:rows, :] = (iga[0:rows, :] + xin[1]) + from_gate
    results[1].start()
    collect(last)
    if slot(last)[0] != 0:
        deliver(last).start()
    for m in range(1, n_dp):
        to_peer(m).wait_recv()
    total = ar_dp[0]
    for m in range(1, n_dp):
        total = total + ar_dp[m]
    ar_z[z] = total
    for dz in range(1, nz):
        to_plane(dz).start()
    for l in range(per_device):
        total = psum[mine[-1 - l] if per_device == 1 else [k for k in mine if slot(k)[1] == l][0]]
        for dz in range(1, nz):
            held = fbuf.at[dz - 1, l, everything]
            remote(psum.at[0, everything], held, f_send.at[0], f_recv.at[dz - 1, l], plane(dz)).wait_recv()
            total = total + fbuf[dz - 1, l]
        gsum_ref[l] = total
    for dz in range(1, nz):
        to_plane(dz).wait_recv()
    total = ar_z[0]
    for dz in range(1, nz):
        total = total + ar_z[dz]
    gg_ref[...] = jnp.concatenate(
        [total[b * PAIRS + p : b * PAIRS + p + 1] for p in range(PAIRS) for b in range(kinds)], axis=0
    )
    for copy in results:
        copy.wait()

    for copy in sends + give_back + [to_sibling]:
        copy.wait_send()
    for m in range(1, n_dp):
        to_peer(m).wait_send()
    for dz in range(1, nz):
        to_plane(dz).wait_send()

    def drain(k, _):
        for copy in scatter(k):
            copy().wait_send()
        return 0

    lax.fori_loop(0, count, drain, 0)

    def drain_z(k, _):
        along(k).wait_send()
        deliver(k).wait_send()
        return 0

    lax.fori_loop(1, late[-1] + 1, drain_z, 0)


def run_experts(features, cotangent, routes_t, lengths, gates_t, first_weight, second_weight, expert_bias):
    rows = features.shape[0]
    n_dp, n_expert = lax.axis_size("dp"), lax.axis_size("expert")
    nz = n_expert // CORES
    per_device, part, _ = first_weight.shape
    height = 2 * part + 8
    count = nz * per_device
    both = CORES * rows
    heads = PAIRS * (BITS + 1)
    hops = n_dp - 1
    gather_hops, sum_hops = (4, 6) if n_dp == 4 else (hops, hops)
    any_spec = pl.BlockSpec(memory_space=pl.ANY)
    vmem = pl.BlockSpec(memory_space=pltpu.VMEM)
    dma = pltpu.SemaphoreType.DMA
    return pl.pallas_call(
        functools.partial(expert_kernel, (rows, n_dp, nz, per_device)),
        out_shape=(
            jax.ShapeDtypeStruct((rows, TASKS * DOUT), F32),
            jax.ShapeDtypeStruct((rows, D), F32),
            jax.ShapeDtypeStruct((per_device, height, D), F32),
            jax.ShapeDtypeStruct((heads, D), F32),
        ),
        in_specs=[any_spec, any_spec, vmem, vmem, vmem, any_spec, any_spec, vmem],
        out_specs=(any_spec, any_spec, vmem, vmem),
        scratch_shapes=[
            pltpu.VMEM((per_device, height, D), F32),
            pltpu.VMEM((2, rows, D), F32),
            pltpu.VMEM((2, rows, TASKS * DOUT), F32),
            pltpu.VMEM((2, 2 * PAIRS, rows), F32),
            pltpu.VMEM((both, 3 * D), BF16),
            pltpu.VMEM((2 * D, both), BF16),
            pltpu.VMEM((both, 4 * DOUT), BF16),
            pltpu.VMEM((4 * DOUT, both), BF16),
            pltpu.VMEM((both, 128), F32),
            pltpu.VMEM((count, both), F32),
            pltpu.VMEM((count, both), F32),
            pltpu.VMEM((both, TASKS * DOUT), F32),
            pltpu.VMEM((both, D), F32),
            pltpu.VMEM((both, 2 * HID), BF16),
            pltpu.VMEM((both, 2 * HID), BF16),
            pltpu.VMEM((3 * D, HID), BF16),
            pltpu.VMEM((2 * HID, D), BF16),
            pltpu.VMEM((2 * HID, DOUT), BF16),
            pltpu.VMEM((2 * DOUT, HID), BF16),
            pltpu.VMEM((count, 8, HID), F32),
            pltpu.VMEM((8, HID), F32),
            pltpu.VMEM((count, 1, DOUT), F32),
            pltpu.VMEM((count, n_dp, height, D), F32),
            pltpu.VMEM((count, hops, height, D), F32),
            pltpu.VMEM((count, height, D), F32),
            pltpu.VMEM((nz - 1, per_device, height, D), F32),
            pltpu.VMEM((PAIRS, rows), F32),
            pltpu.VMEM((PAIRS, rows), F32),
            pltpu.VMEM((2 + BITS, PAIRS, rows), F32),
            pltpu.VMEM((heads, D), F32),
            pltpu.VMEM((heads, D), F32),
            pltpu.VMEM((n_dp, heads, D), F32),
            pltpu.VMEM((nz, heads, D), F32),
            dma((2 + 3 * per_device,)),
            dma((6,)),
            dma((6,)),
            dma((count,)),
            dma((count,)),
            dma((count, gather_hops)),
            dma((count, gather_hops)),
            dma((count, sum_hops)),
            dma((count, sum_hops)),
            dma((count,)),
            dma((nz - 1, per_device)),
            dma((n_dp + nz - 1,)),
            dma((n_dp + nz - 1,)),
            pltpu.SemaphoreType.REGULAR,
        ],
        compiler_params=pltpu.CompilerParams(
            collective_id=0, has_side_effects=True, vmem_limit_bytes=60 << 20
        ),
    )(features, cotangent, routes_t, lengths, gates_t, first_weight, second_weight, expert_bias)


def update_kernel(scale, out_raw, ig_raw, gsum, gg, *refs):
    weights, outs = refs[:12], refs[14:26]
    out_ref, ig_ref = refs[12:14]
    out_held, ig_held, load_sem, store_sem = refs[26:]
    loads, stores = [], []
    for n, (src, held, dst) in enumerate([(out_raw, out_held, out_ref), (ig_raw, ig_held, ig_ref)]):
        step = src.shape[0] // PIECES
        for i in range(PIECES):
            rs = pl.ds(i * step, step)
            loads.append(pltpu.make_async_copy(src.at[rs], held.at[rs], load_sem.at[n, i]))
            stores.append(pltpu.make_async_copy(held.at[rs], dst.at[rs], store_sem.at[n, i]))
    for copy in loads:
        copy.start()
    per_device, part, _ = weights[3].shape
    width = weights[9].shape[1]
    dp = lax.axis_index("dp")
    bias_grad = []
    for l in range(per_device):
        mine = jnp.zeros((1, width), F32)
        for q in range(2 * HID // width):
            row, lane = q * width // HID, q * width % HID
            mine = jnp.where(dp == q, gsum[l, 2 * part + row : 2 * part + row + 1, lane : lane + width], mine)
        bias_grad.append(mine)
    grads = [
        (gg[...], GATE_RATE),
        (gsum[:, 0:part], EXPERT_RATE),
        (gsum[:, part : 2 * part], EXPERT_RATE),
        (jnp.concatenate(bias_grad, axis=0), EXPERT_RATE),
    ]
    for n, (gradient, rate) in enumerate(grads):
        weight, momentum, average = weights[3 * n : 3 * n + 3]
        news = update(weight[...], gradient * scale, momentum[...], average[...], rate)
        for ref, value in zip(outs[3 * n : 3 * n + 3], news):
            ref[...] = value
    for load, store in zip(loads, stores):
        load.wait()
        store.start()
    for copy in stores:
        copy.wait()


def run_updates(scale, out_raw, ig_raw, gsum, gg, weights):
    any_spec = pl.BlockSpec(memory_space=pl.ANY)
    vmem = pl.BlockSpec(memory_space=pltpu.VMEM)
    shapes = [out_raw, ig_raw] + [weights[3 * (n // 3)] for n in range(12)]
    return pl.pallas_call(
        functools.partial(update_kernel, scale),
        out_shape=tuple(jax.ShapeDtypeStruct(array.shape, F32) for array in shapes),
        in_specs=[any_spec, any_spec] + [vmem] * 14,
        out_specs=(any_spec, any_spec) + (vmem,) * 12,
        scratch_shapes=[
            pltpu.VMEM(out_raw.shape, F32),
            pltpu.VMEM(ig_raw.shape, F32),
            pltpu.SemaphoreType.DMA((2, PIECES)),
            pltpu.SemaphoreType.DMA((2, PIECES)),
        ],
    )(out_raw, ig_raw, gsum, gg, *weights)


def local(
    features,
    cotangent,
    routes,
    lengths,
    gate_weight,
    first_weight,
    second_weight,
    expert_bias,
    gate_momentum,
    gate_average,
    first_momentum,
    first_average,
    second_momentum,
    second_average,
    bias_momentum,
    bias_average,
):
    out_raw, ig_raw, gsum, gg = run_experts(
        features, cotangent, routes.T, lengths, gate_weight.T, first_weight, second_weight, expert_bias
    )
    row_count = features.shape[0] * lax.axis_size("dp") * lax.axis_size("expert")
    results = run_updates(
        1.0 / math.sqrt(row_count),
        out_raw,
        ig_raw,
        gsum,
        gg,
        [
            gate_weight.T,
            gate_momentum.T,
            gate_average.T,
            first_weight,
            first_momentum,
            first_average,
            second_weight,
            second_momentum,
            second_average,
            expert_bias,
            bias_momentum,
            bias_average,
        ],
    )
    return (*results[:2], *(value.T for value in results[2:5]), *results[5:])


def solution(mesh):
    rows = P(("dp", "expert"), None)
    weight = P("expert", "dp", None)
    bias = P("expert", "dp")
    return jax.shard_map(
        local,
        mesh=mesh,
        in_specs=(
            rows,
            rows,
            rows,
            rows,
            P(),
            weight,
            weight,
            bias,
            P(),
            P(),
            weight,
            weight,
            weight,
            weight,
            bias,
            bias,
        ),
        out_specs=(
            rows,
            rows,
            P(),
            P(),
            P(),
            weight,
            weight,
            weight,
            weight,
            weight,
            weight,
            bias,
            bias,
            bias,
        ),
        check_vma=False,
    )
```
